32 devices in a mesh: scen: 2 (over x), tm: 16 (over z, y, core).
Axes of the slice: x: 2, y: 2, z: 4, core: 2. Of those that a mesh axis runs over, the one named last changes fastest.
Arguments:
- states: bfloat16 [64, 384], P(('scen', 'tm')), parts along dimension 0, may hold values from -6 to 6
- gradient: float32 [64, 384], P(('scen', 'tm')), parts along dimension 0, may hold values from -0.1 to 0.1
- active_mask: int32 [64, 384], P(('scen', 'tm')), parts along dimension 0, may hold values 0 or 1
- zone_weight: float32 [64, 16], P(('scen', 'tm')), parts along dimension 0, may hold values from 0.001 to 0.004
- zone_map: int32 [768], P('scen'), parts along dimension 0, may hold values from 0 to 15
- w_in: bfloat16 [384, 2048], P('tm'), may hold values from -0.3125 to 0.3125
- w_out: bfloat16 [2048, 384], replicated, may hold values from -0.0625 to 0.0625
- bias: float32 [2048], replicated, may hold values from -3 to 3
Outputs:
- step: float32 [64, 384], P(('scen', 'tm')), parts along dimension 0
The draws below stay inside these ranges and needn't reach their ends.
There are 2 independent parts, one for each index of `scen`. The reference program is written for one: setup_inputs(seed, part) draws one part's arguments, and reference() takes and returns one part's arrays. A program takes and returns all parts, laid end to end along the dimension named above; an argument that names none is the same for every part. Nothing has to cross between parts.
Inputs may be any that keep to these rules, and one draw needn't show every extreme that they name: `zone_map`: each entry names one of the 16 zones.
All inputs are finite; a program needn't handle non-finite values. No bound on the sum of `active_mask` on one device may be relied on, other than what follows from the above.
Results may differ from the reference program's by a relative error of at most 0.0035.
Values may be sent and summed in bfloat16 or wider, within the bound.
A program may use at most 128 MiB of HBM per device.

```python
import math
import jax
import jax.numpy as jnp
from jax import lax

S = 384
H = 2048
ZONES = 16
SECTIONS = 32


def draw_gradient(key, part):
    base = jax.random.normal(key, (SECTIONS, S), jnp.float32) * 0.02
    return jnp.clip(base, -0.1, 0.1)


def place_ends(values, stream_key, least, high):
    longest = values.shape.index(max(values.shape))
    spots = []
    for shift in (0, 1):
        where = [jax.random.randint(jax.random.fold_in(stream_key, axis), (), 0, length) for axis, length in enumerate(values.shape)]
        where[longest] = (where[longest] + shift) % values.shape[longest]
        spots.append(tuple(where))
    return values.at[spots[0]].set(least).at[spots[1]].set(high)


def block_scale(key, shape, cuts, least, high):
    level = 1.0
    for axis_at, shards_of in cuts:
        steps = jax.random.uniform(jax.random.fold_in(jax.random.fold_in(key, 6), axis_at), (shards_of,), jnp.float32, least / len(cuts), high / len(cuts))
        level = level * jnp.repeat(jnp.exp(steps), shape[axis_at] // shards_of).reshape((-1,) + (1,) * (len(shape) - 1 - axis_at))
    return level


def centred(stream_key, extent, scale, most, pieces=(), kind=jnp.bfloat16):
    level = block_scale(stream_key, extent, pieces, -0.22, 0.18) if pieces else 1.0
    drawn = jax.random.normal(stream_key, extent, jnp.float32) * scale * level
    return jnp.minimum(jnp.maximum(drawn, -most), most).astype(kind)


def setup_inputs(seed: int = 0, part: int = 0) -> dict:
    key_list = jax.random.split(jax.random.key(seed), 9)
    part_keys = jax.random.split(jax.random.fold_in(key_list[8], part), 9)
    return {
        "states": centred(part_keys[0], (SECTIONS, S), 1.0, 6.0, ((0, 16),)),
        "gradient": draw_gradient(jax.random.fold_in(jax.random.fold_in(key_list[8], part), 71), part),
        "active_mask": place_ends((jax.random.randint(part_keys[2], (SECTIONS, S), 0, 4) < 1).astype(jnp.int32), jax.random.fold_in(part_keys[2], 1), 0, 1),
        "zone_weight": jnp.clip(jnp.exp(math.log(0.004) - 1.3862944 * jax.random.uniform(part_keys[3], (SECTIONS, ZONES), jnp.float32) ** block_scale(part_keys[3], (SECTIONS, ZONES), ((0, 16),), -0.2, 0.2)), 0.001, 0.004),
        "zone_map": place_ends(jax.random.randint(part_keys[4], (S,), 0, ZONES), jax.random.fold_in(part_keys[4], 1), 0, ZONES - 1).astype(jnp.int32),
        "w_in": centred(key_list[5], (S, H), S ** -0.5, 0.3125, ((0, 16),)),
        "w_out": centred(key_list[6], (H, S), (4 * H) ** -0.5, 0.0625),
        "bias": centred(key_list[7], (H,), 0.5, 3.0, (), jnp.float32),
    }


RHO = 1.0

def matmul(left, right):
    return jnp.dot(left, right, precision=lax.Precision.HIGHEST)

def inverse_factor(matrix):
    width = matrix.shape[0]
    factor = jnp.linalg.cholesky(matrix)
    return jax.scipy.linalg.solve_triangular(factor, jnp.eye(width, dtype=matrix.dtype), lower=True)

def merge_pair(lower, upper):
    middle = lower[2] + upper[0]
    middle_rhs = lower[4] + upper[3]
    inverse = inverse_factor(middle)
    left_solved = matmul(inverse, lower[1].T)
    right_solved = matmul(inverse, upper[1])
    rhs_solved = matmul(inverse, middle_rhs)
    first_first = lower[0] - matmul(left_solved.T, left_solved)
    first_last = -matmul(left_solved.T, right_solved)
    last_last = upper[2] - matmul(right_solved.T, right_solved)
    first_rhs = lower[3] - matmul(left_solved.T, rhs_solved)
    last_rhs = upper[4] - matmul(right_solved.T, rhs_solved)
    return ((first_first, first_last, last_last, first_rhs, last_rhs), (inverse, left_solved, right_solved, rhs_solved))

def back_solve(store, outer_first, outer_last):
    inverse, left_solved, right_solved, rhs_solved = store
    value = rhs_solved - matmul(left_solved, outer_first) - matmul(right_solved, outer_last)
    return matmul(inverse.T, value)

def element_blocks(jacobian, weight_row, grad_row):
    width = jacobian.shape[0]
    first_first = jnp.diag(weight_row) + RHO * matmul(jacobian, jacobian.T)
    first_last = -RHO * jacobian
    last_last = RHO * jnp.eye(width, dtype=jnp.float32)
    return (first_first, first_last, last_last, grad_row, jnp.zeros_like(grad_row))

def solve_ends(chain):
    width = chain[0].shape[0]
    top = jnp.concatenate([chain[0], chain[1]], axis=1)
    bottom = jnp.concatenate([chain[1].T, chain[2]], axis=1)
    system = jnp.concatenate([top, bottom], axis=0)
    inverse = inverse_factor(system)
    rhs = jnp.concatenate([chain[3], chain[4]])
    ends = matmul(inverse.T, matmul(inverse, rhs))
    return (ends[:width], ends[width:])

def reference(states, gradient, active_mask, zone_weight, zone_map, w_in, w_out, bias):
    hidden_in = jnp.dot(states.astype(jnp.float32), w_in.astype(jnp.float32), preferred_element_type=jnp.float32) + bias
    slopes = (1.0 - jnp.tanh(hidden_in) ** 2).astype(jnp.bfloat16)

    def one_section(slope):
        weighted = w_in * slope[None, :]
        product = jnp.dot(weighted.astype(jnp.float32), w_out.astype(jnp.float32), preferred_element_type=jnp.float32)
        return product + jnp.eye(S, dtype=jnp.float32)
    jacobians = lax.map(one_section, slopes)
    weights = zone_weight[:, zone_map] * (1.0 + 4.0 * active_mask.astype(jnp.float32))
    elements = jax.vmap(element_blocks)(jacobians, weights, gradient)
    first = jax.tree.map(lambda part_array: part_array[0], elements)
    rest = jax.tree.map(lambda part_array: part_array[1:], elements)

    def fold(carry, item):
        merged, store = merge_pair(carry, item)
        return (merged, store)
    chain, stores = lax.scan(fold, first, rest)
    start_state, end_state = solve_ends(chain)

    def backward(outer_last, store):
        middle = back_solve(store, start_state, outer_last)
        return (middle, middle)
    _, middles = lax.scan(backward, end_state, stores, reverse=True)
    return jnp.concatenate([start_state[None, :], middles], axis=0)
```

```python
import jax
import jax.numpy as jnp
from jax import lax
from jax.experimental import pallas as pl
from jax.experimental.pallas import tpu as pltpu
from jax.sharding import PartitionSpec as P


def from_partner(array, axis, bit):
    return lax.ppermute(array, axis, [(i, i ^ 1 << bit) for i in range(lax.axis_size(axis))])


def matmul(left, right):
    return jnp.dot(left, right, precision=lax.Precision.HIGHEST)


def dot_exact(left, right, dims=((1,), (0,))):
    return lax.dot_general(
        left, right, (dims, ((), ())), precision=lax.Precision.HIGHEST, preferred_element_type=jnp.float32
    )


def dot_fast(left, right):
    return jnp.dot(
        left.astype(jnp.bfloat16), right.astype(jnp.bfloat16), preferred_element_type=jnp.float32
    )


def invert_in_place(m_ref, x_ref, e_ref):
    width = m_ref.shape[0]
    row_ids = lax.broadcasted_iota(jnp.int32, (width, width), 0)
    col_ids = lax.broadcasted_iota(jnp.int32, (width, width), 1)
    diagonal = row_ids == col_ids
    matrix = m_ref[...]
    square = dot_fast(matrix, matrix)
    trace = jnp.sum(jnp.where(diagonal, matrix, 0.0))
    frobenius = jnp.sum(matrix * matrix)
    bound = jnp.max(jnp.sum(jnp.abs(square), axis=1))
    scale = jnp.minimum(trace / frobenius, 1.9 * lax.rsqrt(bound))
    x_ref[...] = jnp.where(diagonal, 2.0 * scale, 0.0) - (scale * scale) * matrix
    first = jnp.where(diagonal, 1.0, 0.0) - (2.0 * scale) * matrix + (scale * scale) * square
    e_ref[...] = first

    def coarse_step(carry):
        count, _ = carry
        x_ref[...] = x_ref[...] + dot_fast(x_ref[...], e_ref[...])
        residual = jnp.where(diagonal, 1.0, 0.0) - dot_fast(m_ref[...], x_ref[...])
        e_ref[...] = residual
        return count + 1, jnp.sum(residual * residual)

    lax.while_loop(lambda c: (c[0] < 10) & (c[1] > 0.25), coarse_step, (0, jnp.sum(first * first)))

    def fine_step(carry):
        count, _ = carry
        residual = jnp.where(diagonal, 1.0, 0.0) - dot_exact(m_ref[...], x_ref[...])
        x_ref[...] = x_ref[...] + dot_exact(x_ref[...], residual)
        return count + 1, jnp.sum(residual * residual)

    _, last = lax.while_loop(
        lambda c: (c[0] < 12) & jnp.logical_not(c[1] <= 1e-7), fine_step, (0, jnp.float32(1.0))
    )

    @pl.when(jnp.logical_not(last <= 1e-7))
    def _():
        x_ref[...] = m_ref[...]

        def pivot_step(k, carry):
            current = x_ref[...]
            row = x_ref[pl.ds(k, 1), :]
            column = jnp.sum(jnp.where(col_ids == k, current, 0.0), axis=1, keepdims=True)
            pivot = jnp.sum(jnp.where(col_ids[:1] == k, row, 0.0), axis=1, keepdims=True)
            scaled = row / pivot
            updated = jnp.where(col_ids == k, -column / pivot, current - column * scaled)
            own_row = jnp.where(col_ids == k, 1.0 / pivot, scaled)
            x_ref[...] = jnp.where(row_ids == k, own_row, updated)
            return carry

        lax.fori_loop(0, width, pivot_step, 0)


def eliminate_kernel(
    m_ref, mr_ref, l_ref, r_ref, ff_ref, ll_ref, fr_ref, lr_ref,
    off_ref, ofl_ref, oll_ref, ofr_ref, olr_ref, gl_ref, gr_ref, gs_ref, x_ref, e_ref
):
    width = m_ref.shape[0]
    invert_in_place(m_ref, x_ref, e_ref)
    inverse = x_ref[...]
    left = l_ref[...]
    right = r_ref[...]
    gl_ref[...] = dot_exact(left, inverse)
    gr_ref[...] = dot_exact(inverse, right)
    solved = dot_exact(jnp.broadcast_to(mr_ref[...], (8, width)), inverse)
    gs_ref[...] = solved[:1]
    off_ref[...] = ff_ref[...] - dot_exact(gl_ref[...], left, ((1,), (1,)))
    ofl_ref[...] = -dot_exact(gl_ref[...], right)
    oll_ref[...] = ll_ref[...] - dot_exact(jnp.transpose(right), gr_ref[...])
    ofr_ref[...] = fr_ref[...] - dot_exact(solved, left, ((1,), (1,)))[:1]
    olr_ref[...] = lr_ref[...] - dot_exact(solved, right)[:1]


def eliminate(*parts):
    width = parts[0].shape[0]
    full = jax.ShapeDtypeStruct((width, width), jnp.float32)
    row = jax.ShapeDtypeStruct((1, width), jnp.float32)
    result = pl.pallas_call(
        eliminate_kernel,
        out_shape=(full, full, full, row, row, full, full, row),
        scratch_shapes=[pltpu.VMEM((width, width), jnp.float32)] * 2,
        compiler_params=pltpu.CompilerParams(vmem_limit_bytes=48 << 20),
        name="eliminate",
    )(*[part if part.ndim == 2 else part[None] for part in parts])
    return result[:5], result[5:]


def root_kernel(m_ref, mr_ref, o_ref, x_ref, e_ref):
    invert_in_place(m_ref, x_ref, e_ref)
    o_ref[...] = dot_exact(jnp.broadcast_to(mr_ref[...], (8, m_ref.shape[0])), x_ref[...])[:1]


def root_solve(matrix, rhs):
    width = matrix.shape[0]
    return pl.pallas_call(
        root_kernel,
        out_shape=jax.ShapeDtypeStruct((1, width), jnp.float32),
        scratch_shapes=[pltpu.VMEM((width, width), jnp.float32)] * 2,
        compiler_params=pltpu.CompilerParams(vmem_limit_bytes=48 << 20),
        name="root",
    )(matrix, rhs)


def per_device(states, gradient, active_mask, zone_weight, zone_map, w_in, w_out, bias):
    width = states.shape[1]
    devices = lax.axis_size("tm")
    place = lax.axis_index("tm")
    is_first = place == 0
    is_last = place == devices - 1
    zone_count = zone_weight.shape[1]
    zone_table = (
        zone_map[None, :] == lax.broadcasted_iota(jnp.int32, (zone_count, width), 0)
    ).astype(jnp.float32)
    weights = jnp.dot(zone_weight, zone_table, precision=lax.Precision.HIGHEST) * (
        1.0 + 4.0 * active_mask.astype(jnp.float32)
    )
    later = jnp.stack([states[1].astype(jnp.float32), gradient[1], weights[1]])
    before = lax.ppermute(later, "tm", [(i, i + 1) for i in range(devices - 1)])
    whole_rows = lax.all_gather(w_in, "tm", axis=0, tiled=True)
    rows = jnp.stack([before[0].astype(jnp.bfloat16), states[0]])
    hidden_in = jnp.dot(rows, whole_rows, preferred_element_type=jnp.float32) + bias
    slopes = (1.0 - jnp.tanh(hidden_in) ** 2).astype(jnp.bfloat16)
    weighted = slopes[:, None, :] * whole_rows[None, :, :]
    flat = weighted.reshape(2 * width, whole_rows.shape[1])
    product = jnp.dot(flat, w_out, preferred_element_type=jnp.float32).reshape(2, width, width)
    eye = jnp.eye(width, dtype=jnp.float32)
    jac_before = product[0] + eye
    jac_own = product[1] + eye
    last_diag = 1.0 / (1.0 + weights[1])
    column_scale = jnp.where(is_last, weights[1] * last_diag, 1.0)
    tail = jnp.where(is_last, gradient[1] * last_diag, 0.0)
    middle = (
        jnp.diag(weights[0] + jnp.where(is_first, 0.0, 1.0))
        + matmul(jac_own * column_scale[None, :], jac_own.T)
    )
    middle_rhs = gradient[0] + matmul(jac_own, tail)
    left = jnp.where(is_first, 0.0, -jac_before)
    right = jnp.where(is_last, 0.0, -jac_own)
    first_first = jnp.diag(before[2]) + matmul(left, left.T)
    own, local_store = eliminate(
        middle, middle_rhs, left, right, first_first, eye, before[1], jnp.zeros_like(middle_rhs)
    )
    level_count = devices.bit_length() - 1
    level_stores = []
    for level in range(level_count):
        upper_flag = jnp.bitwise_and(jnp.right_shift(place, level), 1) == 1
        if level == level_count - 1:
            block = jnp.where(upper_flag, own[0], own[2])
            vector = jnp.where(upper_flag, own[3], own[4])
            other_block, other_vector = from_partner((block, vector), "tm", level)
            root = root_solve(block + other_block, vector + other_vector)[0]
            break
        partner = from_partner(own, "tm", level)
        lower = [jnp.where(upper_flag, a, b) for a, b in zip(partner, own)]
        upper = [jnp.where(upper_flag, b, a) for a, b in zip(partner, own)]
        own, store = eliminate(
            lower[2] + upper[0], lower[4] + upper[3], lower[1], upper[1],
            lower[0], upper[2], lower[3], upper[4],
        )
        level_stores.append((store, upper_flag))
    top_flag = jnp.right_shift(place, level_count - 1) == 1
    start = jnp.where(top_flag, root, 0.0)
    end = jnp.where(top_flag, 0.0, root)
    for store, upper_flag in reversed(level_stores):
        value = back_solve(store, start, end)
        start = jnp.where(upper_flag, value, start)
        end = jnp.where(upper_flag, end, value)
    value = back_solve(local_store, start, end)
    end = jnp.where(is_last, tail + last_diag * matmul(value, jac_own), end)
    return jnp.stack([value, end], axis=0)


def back_solve(store, outer_first, outer_last):
    left_solved, right_solved, rhs_solved = store
    return rhs_solved[0] - matmul(outer_first, left_solved) - matmul(right_solved, outer_last)


def solution(mesh):
    return jax.shard_map(
        per_device,
        mesh=mesh,
        in_specs=(
            P(("scen", "tm"), None),
            P(("scen", "tm"), None),
            P(("scen", "tm"), None),
            P(("scen", "tm"), None),
            P("scen"),
            P("tm", None),
            P(),
            P(),
        ),
        out_specs=P(("scen", "tm"), None),
        check_vma=False,
    )
```

```python
import jax
import jax.numpy as jnp
from jax import lax
from jax.experimental import pallas as pl
from jax.experimental.pallas import tpu as pltpu
from jax.sharding import PartitionSpec as P


def from_partner(array, axis, bit):
    return lax.ppermute(array, axis, [(i, i ^ 1 << bit) for i in range(lax.axis_size(axis))])


def matmul(left, right):
    return jnp.dot(left, right, precision=lax.Precision.HIGHEST)


def dot_exact(left, right, dims=((1,), (0,))):
    return lax.dot_general(
        left, right, (dims, ((), ())), precision=lax.Precision.HIGHEST, preferred_element_type=jnp.float32
    )


def dot_fast(left, right):
    return jnp.dot(
        left.astype(jnp.bfloat16), right.astype(jnp.bfloat16), preferred_element_type=jnp.float32
    )


def invert_in_place(m_ref, x_ref, e_ref):
    width = m_ref.shape[0]
    row_ids = lax.broadcasted_iota(jnp.int32, (width, width), 0)
    col_ids = lax.broadcasted_iota(jnp.int32, (width, width), 1)
    diagonal = row_ids == col_ids
    matrix = m_ref[...]
    square = dot_fast(matrix, matrix)
    trace = jnp.sum(jnp.where(diagonal, matrix, 0.0))
    frobenius = jnp.sum(matrix * matrix)
    bound = jnp.max(jnp.sum(jnp.abs(square), axis=1))
    scale = jnp.minimum(trace / frobenius, 1.9 * lax.rsqrt(bound))
    x_ref[...] = jnp.where(diagonal, 2.0 * scale, 0.0) - (scale * scale) * matrix
    first = jnp.where(diagonal, 1.0, 0.0) - (2.0 * scale) * matrix + (scale * scale) * square
    e_ref[...] = first

    def coarse_step(carry):
        count, _ = carry
        x_ref[...] = x_ref[...] + dot_fast(x_ref[...], e_ref[...])
        residual = jnp.where(diagonal, 1.0, 0.0) - dot_fast(m_ref[...], x_ref[...])
        e_ref[...] = residual
        return count + 1, jnp.sum(residual * residual)

    lax.while_loop(lambda c: (c[0] < 10) & (c[1] > 0.25), coarse_step, (0, jnp.sum(first * first)))

    def fine_step(carry):
        count, _ = carry
        residual = jnp.where(diagonal, 1.0, 0.0) - dot_exact(m_ref[...], x_ref[...])
        x_ref[...] = x_ref[...] + dot_fast(x_ref[...], residual)
        return count + 1, jnp.sum(residual * residual)

    _, last = lax.while_loop(
        lambda c: (c[0] < 12) & jnp.logical_not(c[1] <= 1e-7), fine_step, (0, jnp.float32(1.0))
    )

    @pl.when(jnp.logical_not(last <= 1e-7))
    def _():
        x_ref[...] = m_ref[...]

        def pivot_step(k, carry):
            current = x_ref[...]
            row = x_ref[pl.ds(k, 1), :]
            column = jnp.sum(jnp.where(col_ids == k, current, 0.0), axis=1, keepdims=True)
            pivot = jnp.sum(jnp.where(col_ids[:1] == k, row, 0.0), axis=1, keepdims=True)
            scaled = row / pivot
            updated = jnp.where(col_ids == k, -column / pivot, current - column * scaled)
            own_row = jnp.where(col_ids == k, 1.0 / pivot, scaled)
            x_ref[...] = jnp.where(row_ids == k, own_row, updated)
            return carry

        lax.fori_loop(0, width, pivot_step, 0)


def finish(left, right, rhs, ff, ll, fr, lr, x_ref, block_ref, vector_ref, gl_ref, gr_ref, gs_ref):
    width = x_ref.shape[0]
    inverse = x_ref[...]
    gl_ref[...] = dot_exact(left, inverse)
    gr_ref[...] = dot_exact(inverse, right)
    solved = dot_exact(jnp.broadcast_to(rhs, (8, width)), inverse)
    gs_ref[...] = solved[:1]
    block_ref[:width] = ff() - dot_exact(gl_ref[...], left, ((1,), (1,)))
    block_ref[width : 2 * width] = -dot_exact(gl_ref[...], right)
    block_ref[2 * width :] = ll() - dot_exact(jnp.transpose(right), gr_ref[...])
    vector_ref[0:1] = fr - dot_exact(solved, left, ((1,), (1,)))[:1]
    vector_ref[1:2] = lr - dot_exact(solved, right)[:1]


def first_kernel(
    m_ref, mr_ref, l_ref, r_ref, ff_ref, ll_ref, fr_ref, lr_ref,
    block_ref, vector_ref, gl_ref, gr_ref, gs_ref, x_ref, e_ref
):
    invert_in_place(m_ref, x_ref, e_ref)
    finish(
        l_ref[...], r_ref[...], mr_ref[...], lambda: ff_ref[...], lambda: ll_ref[...],
        fr_ref[...], lr_ref[...], x_ref, block_ref, vector_ref, gl_ref, gr_ref, gs_ref
    )


def merge_kernel(
    flag_ref, own_ref, other_ref, ov_ref, pv_ref,
    block_ref, vector_ref, gl_ref, gr_ref, gs_ref, x_ref, e_ref, m_ref
):
    width = x_ref.shape[0]
    is_upper = flag_ref[0] == 1
    spans = [pl.ds(k * width, width) for k in range(3)]

    def lower(k):
        return jnp.where(is_upper, other_ref[spans[k], :], own_ref[spans[k], :])

    def upper(k):
        return jnp.where(is_upper, own_ref[spans[k], :], other_ref[spans[k], :])

    m_ref[...] = lower(2) + upper(0)
    invert_in_place(m_ref, x_ref, e_ref)
    lower_rhs = jnp.where(is_upper, pv_ref[...], ov_ref[...])
    upper_rhs = jnp.where(is_upper, ov_ref[...], pv_ref[...])
    finish(
        lower(1), upper(1), lower_rhs[1:2] + upper_rhs[0:1], lambda: lower(0), lambda: upper(2),
        lower_rhs[0:1], upper_rhs[1:2], x_ref, block_ref, vector_ref, gl_ref, gr_ref, gs_ref
    )


def call_merge(kernel, name, width, parts, scratch, in_specs=None):
    full = jax.ShapeDtypeStruct((width, width), jnp.float32)
    result = pl.pallas_call(
        kernel,
        out_shape=(
            jax.ShapeDtypeStruct((3 * width, width), jnp.float32),
            jax.ShapeDtypeStruct((2, width), jnp.float32),
            full, full, jax.ShapeDtypeStruct((1, width), jnp.float32),
        ),
        in_specs=in_specs or [pl.BlockSpec(memory_space=pltpu.VMEM)] * len(parts),
        scratch_shapes=[pltpu.VMEM((width, width), jnp.float32)] * scratch,
        compiler_params=pltpu.CompilerParams(vmem_limit_bytes=48 << 20),
        name=name,
    )(*parts)
    return result[:2], result[2:]


def eliminate(*parts):
    return call_merge(
        first_kernel, "eliminate", parts[0].shape[0],
        [part if part.ndim == 2 else part[None] for part in parts], 2
    )


def merge(upper_flag, own, other):
    vmem = pl.BlockSpec(memory_space=pltpu.VMEM)
    return call_merge(
        merge_kernel, "merge", own[0].shape[1],
        [upper_flag.astype(jnp.int32)[None], own[0], other[0], own[1], other[1]], 3,
        [pl.BlockSpec(memory_space=pltpu.SMEM)] + [vmem] * 4
    )


def exchange(block, vector, core, level):
    if level == 0:
        return from_partner((block, vector), "tm", level)
    half = block.shape[0] // 2
    share = lax.dynamic_slice_in_dim(block, core * half, half, axis=0)
    received, other_vector = from_partner((share, vector), "tm", level)
    swapped = from_partner(received, "tm", 0)
    other = jnp.where(
        core == 1,
        jnp.concatenate([swapped, received]),
        jnp.concatenate([received, swapped]),
    )
    return other, other_vector


def gather_rows(rows, level_count):
    place = lax.axis_index("tm")
    held = rows[None]
    for level in reversed(range(level_count)):
        other = from_partner(held, "tm", level)
        upper_flag = jnp.bitwise_and(jnp.right_shift(place, level), 1) == 1
        held = jnp.stack([jnp.where(upper_flag, other, held), jnp.where(upper_flag, held, other)])
        held = held.reshape((-1,) + rows.shape)
    bits = held.reshape((2,) * level_count + rows.shape)
    order = tuple(reversed(range(level_count))) + (level_count, level_count + 1)
    return bits.transpose(order).reshape(-1, rows.shape[1])


def root_kernel(m_ref, mr_ref, o_ref, x_ref, e_ref):
    invert_in_place(m_ref, x_ref, e_ref)
    o_ref[...] = dot_exact(jnp.broadcast_to(mr_ref[...], (8, m_ref.shape[0])), x_ref[...])[:1]


def root_solve(matrix, rhs):
    width = matrix.shape[0]
    return pl.pallas_call(
        root_kernel,
        out_shape=jax.ShapeDtypeStruct((1, width), jnp.float32),
        scratch_shapes=[pltpu.VMEM((width, width), jnp.float32)] * 2,
        compiler_params=pltpu.CompilerParams(vmem_limit_bytes=48 << 20),
        name="root",
    )(matrix, rhs)


def per_device(states, gradient, active_mask, zone_weight, zone_map, w_in, w_out, bias):
    width = states.shape[1]
    devices = lax.axis_size("tm")
    place = lax.axis_index("tm")
    is_first = place == 0
    is_last = place == devices - 1
    zone_count = zone_weight.shape[1]
    zone_table = (
        zone_map[None, :] == lax.broadcasted_iota(jnp.int32, (zone_count, width), 0)
    ).astype(jnp.float32)
    weights = jnp.dot(zone_weight, zone_table, precision=lax.Precision.HIGHEST) * (
        1.0 + 4.0 * active_mask.astype(jnp.float32)
    )
    later = jnp.stack([states[1].astype(jnp.float32), gradient[1], weights[1]])
    before = lax.ppermute(later, "tm", [(i, i + 1) for i in range(devices - 1)])
    whole_rows = gather_rows(w_in, devices.bit_length() - 1)
    rows = jnp.stack([before[0].astype(jnp.bfloat16), states[0]])
    hidden_in = jnp.dot(rows, whole_rows, preferred_element_type=jnp.float32) + bias
    slopes = (1.0 - jnp.tanh(hidden_in) ** 2).astype(jnp.bfloat16)
    weighted = slopes[:, None, :] * whole_rows[None, :, :]
    flat = weighted.reshape(2 * width, whole_rows.shape[1])
    product = jnp.dot(flat, w_out, preferred_element_type=jnp.float32).reshape(2, width, width)
    eye = jnp.eye(width, dtype=jnp.float32)
    jac_before = product[0] + eye
    jac_own = product[1] + eye
    last_diag = 1.0 / (1.0 + weights[1])
    column_scale = jnp.where(is_last, weights[1] * last_diag, 1.0)
    tail = jnp.where(is_last, gradient[1] * last_diag, 0.0)
    middle = (
        jnp.diag(weights[0] + jnp.where(is_first, 0.0, 1.0))
        + matmul(jac_own * column_scale[None, :], jac_own.T)
    )
    middle_rhs = gradient[0] + matmul(jac_own, tail)
    left = jnp.where(is_first, 0.0, -jac_before)
    right = jnp.where(is_last, 0.0, -jac_own)
    first_first = jnp.diag(before[2]) + matmul(left, left.T)
    own, local_store = eliminate(
        middle, middle_rhs, left, right, first_first, eye, before[1], jnp.zeros_like(middle_rhs)
    )
    core = jnp.bitwise_and(place, 1)
    level_count = devices.bit_length() - 1
    level_stores = []
    for level in range(level_count):
        upper_flag = jnp.bitwise_and(jnp.right_shift(place, level), 1) == 1
        if level == level_count - 1:
            block = jnp.where(upper_flag, own[0][:width], own[0][2 * width :])
            vector = jnp.where(upper_flag, own[1][:1], own[1][1:])
            other_block, other_vector = exchange(block, vector, core, level)
            root = root_solve(block + other_block, vector + other_vector)[0]
            break
        own, store = merge(upper_flag, own, exchange(own[0], own[1], core, level))
        level_stores.append((store, upper_flag))
    top_flag = jnp.right_shift(place, level_count - 1) == 1
    start = jnp.where(top_flag, root, 0.0)
    end = jnp.where(top_flag, 0.0, root)
    for store, upper_flag in reversed(level_stores):
        value = back_solve(store, start, end)
        start = jnp.where(upper_flag, value, start)
        end = jnp.where(upper_flag, end, value)
    value = back_solve(local_store, start, end)
    end = jnp.where(is_last, tail + last_diag * matmul(value, jac_own), end)
    return jnp.stack([value, end], axis=0)


def back_solve(store, outer_first, outer_last):
    left_solved, right_solved, rhs_solved = store
    return rhs_solved[0] - matmul(outer_first, left_solved) - matmul(right_solved, outer_last)


def solution(mesh):
    return jax.shard_map(
        per_device,
        mesh=mesh,
        in_specs=(
            P(("scen", "tm"), None),
            P(("scen", "tm"), None),
            P(("scen", "tm"), None),
            P(("scen", "tm"), None),
            P("scen"),
            P("tm", None),
            P(),
            P(),
        ),
        out_specs=P(("scen", "tm"), None),
        check_vma=False,
    )
```

```python
import jax
import jax.numpy as jnp
from jax import lax
from jax.experimental import pallas as pl
from jax.experimental.pallas import tpu as pltpu
from jax.sharding import PartitionSpec as P


def from_partner(array, axis, bit):
    return lax.ppermute(array, axis, [(i, i ^ 1 << bit) for i in range(lax.axis_size(axis))])


def matmul(left, right):
    return jnp.dot(left, right, precision=lax.Precision.HIGHEST)


def dot_exact(left, right, dims=((1,), (0,))):
    return lax.dot_general(
        left, right, (dims, ((), ())), precision=lax.Precision.HIGHEST, preferred_element_type=jnp.float32
    )


def dot_fast(left, right):
    return jnp.dot(
        left.astype(jnp.bfloat16), right.astype(jnp.bfloat16), preferred_element_type=jnp.float32
    )


def invert_in_place(m_ref, x_ref, e_ref):
    width = m_ref.shape[0]
    row_ids = lax.broadcasted_iota(jnp.int32, (width, width), 0)
    col_ids = lax.broadcasted_iota(jnp.int32, (width, width), 1)
    diagonal = row_ids == col_ids
    matrix = m_ref[...]
    square = dot_fast(matrix, matrix)
    trace = jnp.sum(jnp.where(diagonal, matrix, 0.0))
    frobenius = jnp.sum(matrix * matrix)
    bound = jnp.max(jnp.sum(jnp.abs(square), axis=1))
    scale = jnp.minimum(trace / frobenius, 1.9 * lax.rsqrt(bound))
    x_ref[...] = jnp.where(diagonal, 2.0 * scale, 0.0) - (scale * scale) * matrix
    first = jnp.where(diagonal, 1.0, 0.0) - (2.0 * scale) * matrix + (scale * scale) * square
    e_ref[...] = first

    def coarse_step(carry):
        count, _ = carry
        x_ref[...] = x_ref[...] + dot_fast(x_ref[...], e_ref[...])
        residual = jnp.where(diagonal, 1.0, 0.0) - dot_fast(m_ref[...], x_ref[...])
        e_ref[...] = residual
        return count + 1, jnp.sum(residual * residual)

    lax.while_loop(lambda c: (c[0] < 10) & (c[1] > 0.25), coarse_step, (0, jnp.sum(first * first)))

    def fine_step(carry):
        count, _ = carry
        residual = jnp.where(diagonal, 1.0, 0.0) - dot_exact(m_ref[...], x_ref[...])
        x_ref[...] = x_ref[...] + dot_fast(x_ref[...], residual)
        return count + 1, jnp.sum(residual * residual)

    _, last = lax.while_loop(
        lambda c: (c[0] < 12) & jnp.logical_not(c[1] <= 1e-7), fine_step, (0, jnp.float32(1.0))
    )

    @pl.when(jnp.logical_not(last <= 1e-7))
    def _():
        x_ref[...] = m_ref[...]

        def pivot_step(k, carry):
            current = x_ref[...]
            row = x_ref[pl.ds(k, 1), :]
            column = jnp.sum(jnp.where(col_ids == k, current, 0.0), axis=1, keepdims=True)
            pivot = jnp.sum(jnp.where(col_ids[:1] == k, row, 0.0), axis=1, keepdims=True)
            scaled = row / pivot
            updated = jnp.where(col_ids == k, -column / pivot, current - column * scaled)
            own_row = jnp.where(col_ids == k, 1.0 / pivot, scaled)
            x_ref[...] = jnp.where(row_ids == k, own_row, updated)
            return carry

        lax.fori_loop(0, width, pivot_step, 0)


def unpack_first(packed, row_ids, col_ids):
    return jnp.where(row_ids <= col_ids, packed, jnp.transpose(packed))


def unpack_last(packed, diagonal, row_ids, col_ids):
    whole = jnp.where(row_ids > col_ids, packed, jnp.transpose(packed))
    return jnp.where(row_ids == col_ids, diagonal, whole)


def finish(left, right, rhs, ff, ll, fr, lr, x_ref, block_ref, vector_ref, gl_ref, gr_ref, gs_ref):
    width = x_ref.shape[0]
    inverse = x_ref[...]
    gl_ref[...] = dot_exact(left, inverse)
    gr_ref[...] = dot_exact(inverse, right)
    solved = dot_exact(jnp.broadcast_to(rhs, (8, width)), inverse)
    gs_ref[...] = solved[:1]
    row_ids = lax.broadcasted_iota(jnp.int32, (width, width), 0)
    col_ids = lax.broadcasted_iota(jnp.int32, (width, width), 1)
    new_ff = ff() - dot_exact(gl_ref[...], left, ((1,), (1,)))
    block_ref[width : 2 * width] = -dot_exact(gl_ref[...], right)
    new_ll = ll() - dot_exact(jnp.transpose(right), gr_ref[...])
    block_ref[:width] = jnp.where(row_ids <= col_ids, new_ff, new_ll)
    vector_ref[2:3] = jnp.sum(jnp.where(row_ids == col_ids, new_ll, 0.0), axis=0, keepdims=True)
    vector_ref[0:1] = fr - dot_exact(solved, left, ((1,), (1,)))[:1]
    vector_ref[1:2] = lr - dot_exact(solved, right)[:1]


def first_kernel(
    m_ref, mr_ref, l_ref, r_ref, ff_ref, ll_ref, fr_ref, lr_ref,
    block_ref, vector_ref, gl_ref, gr_ref, gs_ref, x_ref, e_ref
):
    invert_in_place(m_ref, x_ref, e_ref)
    finish(
        l_ref[...], r_ref[...], mr_ref[...], lambda: ff_ref[...], lambda: ll_ref[...],
        fr_ref[...], lr_ref[...], x_ref, block_ref, vector_ref, gl_ref, gr_ref, gs_ref
    )


def merge_kernel(
    flag_ref, own_ref, other_ref, ov_ref, pv_ref,
    block_ref, vector_ref, gl_ref, gr_ref, gs_ref, x_ref, e_ref, m_ref
):
    width = x_ref.shape[0]
    is_upper = flag_ref[0] == 1
    spans = [pl.ds(k * width, width) for k in range(2)]
    row_ids = lax.broadcasted_iota(jnp.int32, (width, width), 0)
    col_ids = lax.broadcasted_iota(jnp.int32, (width, width), 1)
    lower_rhs = jnp.where(is_upper, pv_ref[...], ov_ref[...])
    upper_rhs = jnp.where(is_upper, ov_ref[...], pv_ref[...])

    def lower(k):
        return jnp.where(is_upper, other_ref[spans[k], :], own_ref[spans[k], :])

    def upper(k):
        return jnp.where(is_upper, own_ref[spans[k], :], other_ref[spans[k], :])

    m_ref[...] = unpack_last(lower(0), lower_rhs[2:3], row_ids, col_ids) + unpack_first(
        upper(0), row_ids, col_ids
    )
    invert_in_place(m_ref, x_ref, e_ref)
    finish(
        lower(1), upper(1), lower_rhs[1:2] + upper_rhs[0:1], lambda: unpack_first(lower(0), row_ids, col_ids),
        lambda: unpack_last(upper(0), upper_rhs[2:3], row_ids, col_ids),
        lower_rhs[0:1], upper_rhs[1:2], x_ref, block_ref, vector_ref, gl_ref, gr_ref, gs_ref
    )


def call_merge(kernel, name, width, parts, scratch, in_specs=None):
    full = jax.ShapeDtypeStruct((width, width), jnp.float32)
    result = pl.pallas_call(
        kernel,
        out_shape=(
            jax.ShapeDtypeStruct((2 * width, width), jnp.float32),
            jax.ShapeDtypeStruct((3, width), jnp.float32),
            full, full, jax.ShapeDtypeStruct((1, width), jnp.float32),
        ),
        in_specs=in_specs or [pl.BlockSpec(memory_space=pltpu.VMEM)] * len(parts),
        scratch_shapes=[pltpu.VMEM((width, width), jnp.float32)] * scratch,
        compiler_params=pltpu.CompilerParams(vmem_limit_bytes=48 << 20),
        name=name,
    )(*parts)
    return result[:2], result[2:]


def eliminate(*parts):
    return call_merge(
        first_kernel, "eliminate", parts[0].shape[0],
        [part if part.ndim == 2 else part[None] for part in parts], 2
    )


def merge(upper_flag, own, other):
    vmem = pl.BlockSpec(memory_space=pltpu.VMEM)
    return call_merge(
        merge_kernel, "merge", own[0].shape[1],
        [upper_flag.astype(jnp.int32)[None], own[0], other[0], own[1], other[1]], 3,
        [pl.BlockSpec(memory_space=pltpu.SMEM)] + [vmem] * 4
    )


def exchange(block, vector, core, level):
    if level == 0:
        return from_partner((block, vector), "tm", level)
    half = block.shape[0] // 2
    share = lax.dynamic_slice_in_dim(block, core * half, half, axis=0)
    received, other_vector = from_partner((share, vector), "tm", level)
    swapped = from_partner(received, "tm", 0)
    other = jnp.where(
        core == 1,
        jnp.concatenate([swapped, received]),
        jnp.concatenate([received, swapped]),
    )
    return other, other_vector


def gather_rows(rows, level_count):
    place = lax.axis_index("tm")
    held = rows[None]
    for level in reversed(range(level_count)):
        other = from_partner(held, "tm", level)
        upper_flag = jnp.bitwise_and(jnp.right_shift(place, level), 1) == 1
        held = jnp.stack([jnp.where(upper_flag, other, held), jnp.where(upper_flag, held, other)])
        held = held.reshape((-1,) + rows.shape)
    bits = held.reshape((2,) * level_count + rows.shape)
    order = tuple(reversed(range(level_count))) + (level_count, level_count + 1)
    return bits.transpose(order).reshape(-1, rows.shape[1])


def root_kernel(m_ref, mr_ref, o_ref, x_ref, e_ref):
    invert_in_place(m_ref, x_ref, e_ref)
    o_ref[...] = dot_exact(jnp.broadcast_to(mr_ref[...], (8, m_ref.shape[0])), x_ref[...])[:1]


def root_solve(matrix, rhs):
    width = matrix.shape[0]
    return pl.pallas_call(
        root_kernel,
        out_shape=jax.ShapeDtypeStruct((1, width), jnp.float32),
        scratch_shapes=[pltpu.VMEM((width, width), jnp.float32)] * 2,
        compiler_params=pltpu.CompilerParams(vmem_limit_bytes=48 << 20),
        name="root",
    )(matrix, rhs)


def per_device(states, gradient, active_mask, zone_weight, zone_map, w_in, w_out, bias):
    width = states.shape[1]
    devices = lax.axis_size("tm")
    place = lax.axis_index("tm")
    is_first = place == 0
    is_last = place == devices - 1
    zone_count = zone_weight.shape[1]
    zone_table = (
        zone_map[None, :] == lax.broadcasted_iota(jnp.int32, (zone_count, width), 0)
    ).astype(jnp.float32)
    weights = jnp.dot(zone_weight, zone_table, precision=lax.Precision.HIGHEST) * (
        1.0 + 4.0 * active_mask.astype(jnp.float32)
    )
    later = jnp.stack([states[1].astype(jnp.float32), gradient[1], weights[1]])
    before = lax.ppermute(later, "tm", [(i, i + 1) for i in range(devices - 1)])
    whole_rows = gather_rows(w_in, devices.bit_length() - 1)
    rows = jnp.stack([before[0].astype(jnp.bfloat16), states[0]])
    hidden_in = jnp.dot(rows, whole_rows, preferred_element_type=jnp.float32) + bias
    slopes = (1.0 - jnp.tanh(hidden_in) ** 2).astype(jnp.bfloat16)
    weighted = slopes[:, None, :] * whole_rows[None, :, :]
    flat = weighted.reshape(2 * width, whole_rows.shape[1])
    product = jnp.dot(flat, w_out, preferred_element_type=jnp.float32).reshape(2, width, width)
    eye = jnp.eye(width, dtype=jnp.float32)
    jac_before = product[0] + eye
    jac_own = product[1] + eye
    last_diag = 1.0 / (1.0 + weights[1])
    column_scale = jnp.where(is_last, weights[1] * last_diag, 1.0)
    tail = jnp.where(is_last, gradient[1] * last_diag, 0.0)
    middle = (
        jnp.diag(weights[0] + jnp.where(is_first, 0.0, 1.0))
        + matmul(jac_own * column_scale[None, :], jac_own.T)
    )
    middle_rhs = gradient[0] + matmul(jac_own, tail)
    left = jnp.where(is_first, 0.0, -jac_before)
    right = jnp.where(is_last, 0.0, -jac_own)
    first_first = jnp.diag(before[2]) + matmul(left, left.T)
    own, local_store = eliminate(
        middle, middle_rhs, left, right, first_first, eye, before[1], jnp.zeros_like(middle_rhs)
    )
    core = jnp.bitwise_and(place, 1)
    level_count = devices.bit_length() - 1
    level_stores = []
    for level in range(level_count):
        upper_flag = jnp.bitwise_and(jnp.right_shift(place, level), 1) == 1
        if level == level_count - 1:
            row_ids = lax.broadcasted_iota(jnp.int32, (width, width), 0)
            packed, flipped = own[0][:width], own[0][:width].T
            keep = jnp.where(upper_flag, row_ids <= row_ids.T, row_ids > row_ids.T)
            block = jnp.where(keep, packed, flipped)
            block = jnp.where((row_ids == row_ids.T) & ~upper_flag, own[1][2:3], block)
            vector = jnp.where(upper_flag, own[1][:1], own[1][1:2])
            other_block, other_vector = exchange(block, vector, core, level)
            root = root_solve(block + other_block, vector + other_vector)[0]
            break
        own, store = merge(upper_flag, own, exchange(own[0], own[1], core, level))
        level_stores.append((store, upper_flag))
    top_flag = jnp.right_shift(place, level_count - 1) == 1
    start = jnp.where(top_flag, root, 0.0)
    end = jnp.where(top_flag, 0.0, root)
    for store, upper_flag in reversed(level_stores):
        value = back_solve(store, start, end)
        start = jnp.where(upper_flag, value, start)
        end = jnp.where(upper_flag, end, value)
    value = back_solve(local_store, start, end)
    end = jnp.where(is_last, tail + last_diag * matmul(value, jac_own), end)
    return jnp.stack([value, end], axis=0)


def back_solve(store, outer_first, outer_last):
    left_solved, right_solved, rhs_solved = store
    return rhs_solved[0] - matmul(outer_first, left_solved) - matmul(right_solved, outer_last)


def solution(mesh):
    return jax.shard_map(
        per_device,
        mesh=mesh,
        in_specs=(
            P(("scen", "tm"), None),
            P(("scen", "tm"), None),
            P(("scen", "tm"), None),
            P(("scen", "tm"), None),
            P("scen"),
            P("tm", None),
            P(),
            P(),
        ),
        out_specs=P(("scen", "tm"), None),
        check_vma=False,
    )
```
